768 devices in a mesh: seq: 96 (over z, y), tp: 8 (over x, core).
Axes of the slice: x: 4, y: 8, z: 12, core: 2. Of those that a mesh axis runs over, the one named last changes fastest.
Arguments:
- inputs: bfloat16 [12288, 4096], P('seq', 'tp'), may hold values from -6 to 6
- frozen_query_key_value: bfloat16 [3, 12288, 2048], P(None, 'seq', 'tp'), may hold values from -6 to 6
- adapter_down_maps: bfloat16 [3, 4096, 16], P(None, 'tp'), may hold values from -0.09375 to 0.09375
- adapter_up_maps: bfloat16 [3, 16, 2048], P(None, None, 'tp'), may hold values from -1.5 to 1.5
- incoming_state: float32 [32, 64, 64], P('tp'), may hold values from -1280 to 1280
- output_weight_matrix: bfloat16 [2048, 4096], P('tp'), may hold values from -0.125 to 0.125
- output_down_map: bfloat16 [2048, 16], P('tp'), may hold values from -0.125 to 0.125
- output_up_map: bfloat16 [16, 4096], replicated, may hold values from -1.5 to 1.5
- output_gradient: bfloat16 [12288, 4096], P('seq'), may hold values from -6 to 6
Outputs:
- attended: bfloat16 [12288, 2048], P('seq', 'tp')
- grad_down: float32 [3, 4096, 16], P(None, 'tp')
- grad_up: float32 [3, 16, 2048], P(None, None, 'tp')
- grad_out_down: float32 [2048, 16], P('tp')
- grad_out_up: float32 [16, 4096], replicated
- grad_state: float32 [32, 64, 64], P('tp')
The draws below stay inside these ranges and needn't reach their ends.
All inputs are finite; a program needn't handle non-finite values.
Results may differ from the reference program's by a relative error of at most 0.022.
Values may be sent and summed in bfloat16 or wider, within the bound.
No kernel may reach another device: no remote copies, remote signals or barrier semaphores. Data moves between devices by JAX's collectives and lax.ppermute only.
A program may use at most 64 MiB of HBM per device.

```python
import math
import jax
import jax.numpy as jnp
from jax import lax

MODEL_WIDTH = 4096
HEADS = 32
DH = 64
ADAPTER_RANK = 16
TOK_DEV = 128
ATT_WIDTH = 2048
TOKENS = 12288
N_SEQ = 96
N_TP = 8


def level_of(rng, extent, pieces, low, largest):
    factor_of = 1.0
    for dim, parts in pieces:
        draws = jax.random.uniform(jax.random.fold_in(jax.random.fold_in(rng, 6), dim), (parts,), jnp.float32, low / len(pieces), largest / len(pieces))
        factor_of = factor_of * jnp.repeat(jnp.exp(draws), extent[dim] // parts).reshape((-1,) + (1,) * (len(extent) - 1 - dim))
    return factor_of


def centred(rng, extent, spread, reach, shards=(), held_as=jnp.bfloat16):
    factor_of = level_of(rng, extent, shards, -0.22, 0.18) if shards else 1.0
    entries = jax.random.normal(rng, extent, jnp.float32) * spread * factor_of
    return jnp.minimum(jnp.maximum(entries, -reach), reach).astype(held_as)


def setup_inputs(seed: int = 0) -> dict:
    key_list = jax.random.split(jax.random.key(seed), 10)
    return {
        "inputs": centred(key_list[0], (TOKENS, MODEL_WIDTH), 1.0, 6.0, ((0, 96), (1, 8))),
        "frozen_query_key_value": centred(key_list[1], (3, TOKENS, ATT_WIDTH), 1.0, 6.0, ((1, 96), (2, 8))),
        "adapter_down_maps": centred(key_list[2], (3, MODEL_WIDTH, ADAPTER_RANK), MODEL_WIDTH ** -0.5, 0.09375, ((1, 8),)),
        "adapter_up_maps": centred(key_list[3], (3, ADAPTER_RANK, ATT_WIDTH), ADAPTER_RANK ** -0.5, 1.5, ((2, 8),)),
        "incoming_state": centred(key_list[4], (HEADS, DH, DH), (2.0 * TOKENS ** 0.5), 1280.0, ((0, 8),), jnp.float32),
        "output_weight_matrix": centred(key_list[5], (ATT_WIDTH, MODEL_WIDTH), ATT_WIDTH ** -0.5, 0.125, ((0, 8),)),
        "output_down_map": centred(key_list[6], (ATT_WIDTH, ADAPTER_RANK), ATT_WIDTH ** -0.5, 0.125, ((0, 8),)),
        "output_up_map": centred(key_list[7], (ADAPTER_RANK, MODEL_WIDTH), ADAPTER_RANK ** -0.5, 1.5),
        "output_gradient": centred(key_list[8], (TOKENS, MODEL_WIDTH), 1.0, 6.0, ((0, 96),)),
    }


def block_terms(query_rows, key_rows, value_rows, grad_rows, state, later_sum, scale_factor):
    count = query_rows.shape[0]
    causal = jnp.arange(count)[:, None] >= jnp.arange(count)[None, :]
    queries = query_rows.astype(jnp.float32)
    keys_all = key_rows.astype(jnp.float32)
    values_all = value_rows.astype(jnp.float32)
    grads_all = grad_rows.astype(jnp.float32)
    state_low = state.astype(jnp.bfloat16).astype(jnp.float32)
    later_low = later_sum.astype(jnp.bfloat16).astype(jnp.float32)
    scores = jnp.einsum('thd,shd->hts', queries, keys_all)
    weights = jnp.where(causal[None], scores, 0.0).astype(jnp.bfloat16).astype(jnp.float32)
    result = scale_factor * (jnp.einsum('hts,shd->thd', weights, values_all) + jnp.einsum('thd,hde->the', queries, state_low))
    dscores = jnp.einsum('the,she->hts', grads_all, values_all)
    dweights = jnp.where(causal[None], dscores, 0.0).astype(jnp.bfloat16).astype(jnp.float32)
    grad_query = jnp.einsum('hts,shd->thd', dweights, keys_all) + jnp.einsum('the,hde->thd', grads_all, state_low)
    grad_key = jnp.einsum('hts,thd->shd', dweights, queries) + jnp.einsum('the,hde->thd', values_all, later_low)
    grad_value = jnp.einsum('hts,the->she', weights, grads_all) + jnp.einsum('thd,hde->the', keys_all, later_low)
    return (result.astype(jnp.bfloat16), grad_query.astype(jnp.bfloat16), grad_key.astype(jnp.bfloat16), grad_value.astype(jnp.bfloat16))

def group_sum(partials):
    rounded = lax.optimization_barrier(partials.astype(jnp.bfloat16))
    return lax.optimization_barrier(jnp.sum(rounded.astype(jnp.float32), axis=0)).astype(jnp.bfloat16)

def reference(inputs, frozen_query_key_value, adapter_down_maps, adapter_up_maps, incoming_state, output_weight_matrix, output_down_map, output_up_map, output_gradient):
    scale_factor = 1.0 / math.sqrt(DH * TOKENS)
    group_width = MODEL_WIDTH // N_TP
    att_group = ATT_WIDTH // N_TP
    inputs_grouped = inputs.astype(jnp.float32).reshape(TOKENS, N_TP, group_width)
    down_grouped = adapter_down_maps.astype(jnp.float32).reshape(3, N_TP, group_width, ADAPTER_RANK)
    lowrank_term = group_sum(jnp.einsum('xgo,hgoe->ghxe', inputs_grouped, down_grouped))
    projected_rows = (frozen_query_key_value.astype(jnp.float32) + jnp.einsum('sqm,smg->sqg', lowrank_term.astype(jnp.float32), adapter_up_maps.astype(jnp.float32))).astype(jnp.bfloat16)
    down_grad = jnp.dot(output_gradient, output_up_map.T, preferred_element_type=jnp.float32).astype(jnp.bfloat16)
    grad_att = (scale_factor * (jnp.dot(output_gradient, output_weight_matrix.T, preferred_element_type=jnp.float32) + jnp.dot(down_grad, output_down_map.T, preferred_element_type=jnp.float32))).astype(jnp.bfloat16)
    shaped = (N_SEQ, TOK_DEV, HEADS, DH)
    queries = projected_rows[0].reshape(shaped)
    keys_all = projected_rows[1].reshape(shaped)
    values_all = projected_rows[2].reshape(shaped)
    grads_all = grad_att.reshape(shaped)
    qg_all = jnp.einsum('bthd,bthe->hde', queries.astype(jnp.float32), grads_all.astype(jnp.float32))

    def advance(carry, blocks):
        state, qg_before = carry
        query_rows, key_rows, value_rows, grad_rows = blocks
        kv_own = jnp.einsum('thd,the->hde', key_rows.astype(jnp.float32), value_rows.astype(jnp.float32))
        qg_own = jnp.einsum('thd,the->hde', query_rows.astype(jnp.float32), grad_rows.astype(jnp.float32))
        later_sum = qg_all - qg_before - qg_own
        terms = block_terms(query_rows, key_rows, value_rows, grad_rows, state, later_sum, scale_factor)
        return ((state + kv_own, qg_before + qg_own), terms)
    start = (incoming_state, jnp.zeros_like(incoming_state))
    _, (result, grad_query, grad_key, grad_value) = lax.scan(advance, start, (queries, keys_all, values_all, grads_all))
    attended = result.reshape(TOKENS, ATT_WIDTH)
    gradient_projection = jnp.stack([grad_query, grad_key, grad_value]).reshape(3, TOKENS, ATT_WIDTH)
    grad_up = jnp.stack([jnp.dot(lowrank_term[projection_index].T, gradient_projection[projection_index], preferred_element_type=jnp.float32) for projection_index in range(3)])
    proj_grouped = gradient_projection.astype(jnp.float32).reshape(3, TOKENS, N_TP, att_group)
    up_grouped = adapter_up_maps.astype(jnp.float32).reshape(3, ADAPTER_RANK, N_TP, att_group)
    gradient_lowrank = group_sum(jnp.einsum('itgn,irgn->gitr', proj_grouped, up_grouped))
    grad_down = jnp.stack([jnp.dot(inputs.T, gradient_lowrank[projection_index], preferred_element_type=jnp.float32) for projection_index in range(3)])
    attended_grouped = attended.astype(jnp.float32).reshape(TOKENS, N_TP, att_group)
    out_down_grouped = output_down_map.astype(jnp.float32).reshape(N_TP, att_group, ADAPTER_RANK)
    out_low = group_sum(jnp.einsum('tgn,gnr->gtr', attended_grouped, out_down_grouped))
    grad_out_up = jnp.dot(out_low.T, output_gradient, preferred_element_type=jnp.float32)
    grad_out_down = jnp.dot(attended.T, down_grad, preferred_element_type=jnp.float32)
    return (attended, grad_down, grad_up, grad_out_down, grad_out_up, qg_all)
```

```python
import functools
import math

import jax
import jax.numpy as jnp
from jax import lax
from jax.experimental import pallas as pl
from jax.experimental.pallas import tpu as pltpu
from jax.sharding import PartitionSpec as P

DH = 64
RANK = 16
Y_SIZE = 8
BF = jnp.bfloat16
F32 = jnp.float32


def dot(a, b, contract):
    return lax.dot_general(a, b, ((contract[:1], contract[1:]), ((), ())), preferred_element_type=F32)


NN, NT, TN = (1, 0), (1, 1), (0, 0)


def iota(shape, axis):
    return lax.broadcasted_iota(jnp.int32, shape, axis)


def total(ref):
    acc = ref[0].astype(F32)
    for k in range(1, ref.shape[0]):
        acc = acc + ref[k].astype(F32)
    return acc


def fill(ref, value):
    for k in range(ref.shape[0]):
        ref[k] = value


def sum_spread_kernel(in_ref, out_ref):
    fill(out_ref, total(in_ref).astype(BF))


def low_kernel(x_ref, down_ref, out_ref):
    fill(out_ref, dot(down_ref[...], x_ref[...], NT).astype(BF))


def per_head(rows):
    count, width = rows.shape
    lane = iota((count, width), 1) // DH
    return jnp.concatenate([jnp.where(lane == h, rows, jnp.zeros_like(rows)) for h in range(width // DH)], axis=0)


def project_kernel(
    scale, got_ref, frozen_ref, up_ref, og_ref, w_ref, wd_ref, oup_ref, low_ref, proj_ref, grad_ref, dg_ref, out_ref
):
    width = frozen_ref.shape[2]
    down_grad = dot(oup_ref[...], og_ref[...], NT).astype(BF)
    dg_ref[...] = down_grad
    through = dot(og_ref[...], w_ref[...], NT) + dot(down_grad, wd_ref[...], TN)
    grad = (scale * through).astype(BF)
    grad_ref[...] = grad
    low = total(got_ref).astype(BF)
    low_ref[...] = low
    rows = []
    for i in range(3):
        part = frozen_ref[i].astype(F32) + dot(low[i * RANK : (i + 1) * RANK], up_ref[i], TN)
        rows.append(part.astype(BF))
        proj_ref[i] = rows[i]
    query, key, value = rows
    same = iota((width, width), 0) // DH == iota((width, width), 1) // DH
    kv = jnp.where(same, dot(key, value, TN), 0.0).astype(BF)
    qg = jnp.where(same, dot(query, grad, TN), 0.0).astype(BF)
    column, lane = iota((width, 2 * DH), 0) % DH, iota((width, 2 * DH), 1)
    left = (lane == column).astype(BF)
    right = (lane == column + DH).astype(BF)
    packed = (dot(kv, left, NN) + dot(qg, right, NN)).astype(BF)
    slices = out_ref.shape[0]
    size = width // slices
    for j in range(slices):
        out_ref[j] = packed[j * size : (j + 1) * size]


def scan_kernel(z_ref, planes_ref, blocks_ref, out_ref):
    planes, blocks, size = planes_ref.shape[0], blocks_ref.shape[0], blocks_ref.shape[1]
    mine = z_ref[0]
    first = iota((size, 2 * DH), 1) < DH
    zero = jnp.zeros((size, 2 * DH), F32)
    before, after, whole = zero, zero, zero
    for k in range(planes):
        term = planes_ref[k].astype(F32)
        before = before + jnp.where(k < mine, term, 0.0)
        after = after + jnp.where(k > mine, term, 0.0)
        whole = whole + term
    ahead = [before]
    for k in range(blocks - 1):
        ahead.append(ahead[k] + blocks_ref[k].astype(F32))
    behind = [after]
    for k in range(blocks - 1, 0, -1):
        behind.append(behind[-1] + blocks_ref[k].astype(F32))
    behind = behind[::-1]
    for k in range(blocks):
        out_ref[k, :size] = jnp.where(first, ahead[k], behind[k]).astype(BF)
        out_ref[k, size:] = whole.astype(BF)


def attend_kernel(
    scale,
    got_ref,
    state_ref,
    proj_ref,
    grad_ref,
    low_ref,
    up_ref,
    wd_ref,
    dg_ref,
    att_ref,
    gstate_ref,
    part_ref,
    gup_ref,
):
    slices, size = got_ref.shape[0], got_ref.shape[1] // 2
    rows, width = grad_ref.shape
    heads = width // DH
    sums = jnp.concatenate([got_ref[j, :size] for j in range(slices)], axis=0)
    wholes = jnp.concatenate([got_ref[j, size:] for j in range(slices)], axis=0)
    lane, column = iota((2 * DH, DH), 0), iota((2 * DH, DH), 1)
    tail = (lane == column + DH).astype(BF)
    gstate_ref[...] = dot(wholes, tail, NN)
    state = (sums[:, :DH].astype(F32) + state_ref[...]).astype(BF)
    lane, column = iota((DH, width), 0), iota((DH, width), 1) % DH
    head_spread = (lane == column).astype(BF)
    lane, column = iota((2 * DH, width), 0), iota((2 * DH, width), 1) % DH
    tail_spread = (lane == column + DH).astype(BF)
    same = iota((width, width), 0) // DH == iota((width, width), 1) // DH
    state_low = jnp.where(same, dot(state, head_spread, NN), 0.0).astype(BF)
    later_low = jnp.where(same, dot(sums, tail_spread, NN), 0.0).astype(BF)
    query, key, value, grad = proj_ref[0], proj_ref[1], proj_ref[2], grad_ref[...]
    query_s, key_s, value_s, grad_s = per_head(query), per_head(key), per_head(value), per_head(grad)
    row, col = iota((rows, heads * rows), 0), iota((rows, heads * rows), 1) % rows
    lower, upper = col <= row, col >= row
    weights = jnp.where(lower, dot(query, key_s, NT), 0.0).astype(BF)
    weights_t = jnp.where(upper, dot(key, query_s, NT), 0.0).astype(BF)
    dweights = jnp.where(lower, dot(grad, value_s, NT), 0.0).astype(BF)
    dweights_t = jnp.where(upper, dot(value, grad_s, NT), 0.0).astype(BF)
    attended = (scale * (dot(weights, value_s, NN) + dot(query, state_low, NN))).astype(BF)
    att_ref[...] = attended
    back = (
        (dot(dweights, key_s, NN) + dot(grad, state_low, NT)).astype(BF),
        (dot(dweights_t, query_s, NN) + dot(value, later_low, NT)).astype(BF),
        (dot(weights_t, grad_s, NN) + dot(key, later_low, NN)).astype(BF),
    )
    parts = []
    for i in range(3):
        parts.append(dot(up_ref[i], back[i], NT))
        gup_ref[i * RANK : (i + 1) * RANK] = dot(low_ref[i * RANK : (i + 1) * RANK], back[i], NN).astype(BF)
    parts.append(dot(wd_ref[...], attended, NT))
    gup_ref[3 * RANK :] = dot(dg_ref[...], attended, NN).astype(BF)
    fill(part_ref, jnp.concatenate(parts, axis=0).astype(BF))


def layout(slices, model, cols, width):
    lanes = 128
    out_up = RANK * model // (slices * lanes)
    ups = 4 * RANK * width // (slices * lanes)
    down = 3 * RANK * cols // (slices * lanes)
    return out_up, ups, down


def pieces(slices, model, cols, width):
    out_up, ups, down = layout(slices, model, cols, width)
    span = model // slices
    up_rows = 4 * RANK // slices
    half = 3 * RANK // 2
    units = [(r * half, c * 128) for c in range(cols // 128) for r in range(2)]
    each = len(units) // slices
    found = []
    for j in range(slices):
        for c in range(span // 128):
            found.append((j, c * RANK, RANK, "o", 0, j * span + c * 128))
        for c in range(width // 128):
            for r in range(0, up_rows, 8):
                found.append((j, out_up + c * up_rows + r, 8, "u", j * up_rows + r, c * 128))
        for n in range(each):
            found.append((j, out_up + ups + n * half, half, "d", *units[j * each + n]))
    return found


def grads_kernel(got_ref, x_ref, og_ref, gup_ref, out_ref):
    low = total(got_ref).astype(BF)
    down = dot(low[: 3 * RANK], x_ref[...], NN).astype(BF)
    out_up = dot(low[3 * RANK :], og_ref[...], NN).astype(BF)
    kept = {"o": out_up, "u": gup_ref[...], "d": down}
    for j, at, count, name, row, col in pieces(out_ref.shape[0], og_ref.shape[1], x_ref.shape[1], gup_ref.shape[1]):
        out_ref[j, at : at + count] = kept[name][row : row + count, col : col + 128]


def unpack_kernel(got_ref, down_ref, up_ref, odown_ref, oup_ref):
    slices, model, cols, width = got_ref.shape[0], oup_ref.shape[1], down_ref.shape[1], up_ref.shape[1]
    for j, at, count, name, row, col in pieces(slices, model, cols, width):
        value = got_ref[j, at : at + count].astype(F32)
        if name == "o":
            oup_ref[row : row + count, col : col + 128] = value
        elif name == "d":
            down_ref[row : row + count, col : col + 128] = value
        elif row < 3 * RANK:
            up_ref[row : row + count, col : col + 128] = value
        else:
            odown_ref[row - 3 * RANK : row - 3 * RANK + count, col : col + 128] = value


def run(kernel, outs, *args, scalars=0, limit=16 << 20):
    vmem = pl.BlockSpec(memory_space=pltpu.VMEM)
    smem = pl.BlockSpec(memory_space=pltpu.SMEM)
    return pl.pallas_call(
        kernel,
        out_shape=[jax.ShapeDtypeStruct(shape, dtype) for shape, dtype in outs],
        in_specs=[smem] * scalars + [vmem] * (len(args) - scalars),
        out_specs=[vmem] * len(outs),
        compiler_params=pltpu.CompilerParams(vmem_limit_bytes=limit),
    )(*args)


def on_device(y_size, z_size, tp_size, inputs, frozen, down_maps, up_maps, state, w_out, down_out, up_out, out_grad):
    rows, cols = inputs.shape
    width, model = frozen.shape[2], out_grad.shape[1]
    scale = 1.0 / math.sqrt(DH * rows * y_size * z_size)
    planes = [[z * y_size + y for y in range(y_size)] for z in range(z_size)]
    columns = [[z * y_size + y for z in range(z_size)] for y in range(y_size)]

    def over_y(a):
        return lax.all_to_all(a, "seq", 0, 0, axis_index_groups=planes)

    def over_z(a):
        return lax.all_to_all(a, "seq", 0, 0, axis_index_groups=columns)

    def over_tp(a):
        return lax.all_to_all(a, "tp", 0, 0)

    down_t = jnp.transpose(down_maps, (0, 2, 1)).reshape(3 * RANK, cols)
    wd_t = down_out.T
    z_index = (lax.axis_index("seq") // y_size).reshape(1)

    (low_part,) = run(low_kernel, [((tp_size, 3 * RANK, rows), BF)], inputs, down_t)
    low, proj, grad, down_grad, own = run(
        functools.partial(project_kernel, scale),
        [
            ((3 * RANK, rows), BF),
            ((3, rows, width), BF),
            ((rows, width), BF),
            ((RANK, rows), BF),
            ((y_size, width // y_size, 2 * DH), BF),
        ],
        over_tp(low_part),
        frozen,
        up_maps,
        out_grad,
        w_out,
        wd_t,
        up_out,
    )
    blocks = over_y(own)
    slice_rows = width // y_size
    (plane,) = run(sum_spread_kernel, [((z_size, slice_rows, 2 * DH), BF)], blocks)
    (sums,) = run(
        scan_kernel, [((y_size, 2 * slice_rows, 2 * DH), BF)], z_index, over_z(plane), blocks, scalars=1
    )
    attended, grad_state, parts, grad_up = run(
        functools.partial(attend_kernel, scale),
        [
            ((rows, width), BF),
            ((width, DH), F32),
            ((tp_size, 4 * RANK, rows), BF),
            ((4 * RANK, width), BF),
        ],
        over_y(sums),
        state.reshape(width, DH),
        proj,
        grad,
        low,
        up_maps,
        wd_t,
        down_grad,
    )
    lines = sum(layout(y_size, model, cols, width))
    (shares,) = run(grads_kernel, [((y_size, lines, 128), BF)], over_tp(parts), inputs, out_grad, grad_up)
    (mine,) = run(sum_spread_kernel, [((z_size, lines, 128), BF)], over_y(shares))
    (whole,) = run(sum_spread_kernel, [((y_size, lines, 128), BF)], over_z(mine))
    down_g, up_g, odown_g, oup_g = run(
        unpack_kernel,
        [((3 * RANK, cols), F32), ((3 * RANK, width), F32), ((RANK, width), F32), ((RANK, model), F32)],
        over_y(whole),
    )
    return (
        attended,
        jnp.transpose(down_g.reshape(3, RANK, cols), (0, 2, 1)),
        up_g.reshape(3, RANK, width),
        odown_g.T,
        oup_g,
        grad_state.reshape(width // DH, DH, DH),
    )


def solution(mesh):
    placed = (
        P("seq", "tp"),
        P(None, "seq", "tp"),
        P(None, "tp", None),
        P(None, None, "tp"),
        P("tp", None, None),
        P("tp", None),
        P("tp", None),
        P(),
        P("seq", None),
    )
    seq, tp = mesh.shape["seq"], mesh.shape["tp"]
    return jax.shard_map(
        functools.partial(on_device, Y_SIZE, seq // Y_SIZE, tp),
        mesh=mesh,
        in_specs=placed,
        out_specs=(
            P("seq", "tp"),
            P(None, "tp", None),
            P(None, None, "tp"),
            P("tp", None),
            P(),
            P("tp", None, None),
        ),
        check_vma=False,
    )
```

```python
import functools
import math

import jax
import jax.numpy as jnp
from jax import lax
from jax.experimental import pallas as pl
from jax.experimental.pallas import tpu as pltpu
from jax.sharding import PartitionSpec as P

DH = 64
RANK = 16
Y_SIZE = 8
BF = jnp.bfloat16
F32 = jnp.float32


def dot(a, b, contract):
    return lax.dot_general(a, b, ((contract[:1], contract[1:]), ((), ())), preferred_element_type=F32)


NN, NT, TN = (1, 0), (1, 1), (0, 0)


def iota(shape, axis):
    return lax.broadcasted_iota(jnp.int32, shape, axis)


def total(ref):
    acc = ref[0].astype(F32)
    for k in range(1, ref.shape[0]):
        acc = acc + ref[k].astype(F32)
    return acc


def fill(ref, value):
    for k in range(ref.shape[0]):
        ref[k] = value


def sum_spread_kernel(in_ref, out_ref):
    fill(out_ref, total(in_ref).astype(BF))


def low_kernel(x_ref, down_ref, out_ref):
    fill(out_ref, dot(down_ref[...], x_ref[...], NT).astype(BF))


def per_head(rows):
    count, width = rows.shape
    lane = iota((count, width), 1) // DH
    return jnp.concatenate([jnp.where(lane == h, rows, jnp.zeros_like(rows)) for h in range(width // DH)], axis=0)


def project_kernel(
    scale, got_ref, frozen_ref, up_ref, og_ref, w_ref, wd_ref, oup_ref, low_ref, proj_ref, grad_ref, dg_ref, out_ref
):
    width = frozen_ref.shape[2]
    down_grad = dot(oup_ref[...], og_ref[...], NT).astype(BF)
    dg_ref[...] = down_grad
    through = dot(og_ref[...], w_ref[...], NT) + dot(down_grad, wd_ref[...], TN)
    grad = (scale * through).astype(BF)
    grad_ref[...] = grad
    low = total(got_ref).astype(BF)
    low_ref[...] = low
    rows = []
    for i in range(3):
        part = frozen_ref[i].astype(F32) + dot(low[i * RANK : (i + 1) * RANK], up_ref[i], TN)
        rows.append(part.astype(BF))
        proj_ref[i] = rows[i]
    query, key, value = rows
    same = iota((width, width), 0) // DH == iota((width, width), 1) // DH
    kv = jnp.where(same, dot(key, value, TN), 0.0).astype(BF)
    qg = jnp.where(same, dot(query, grad, TN), 0.0).astype(BF)
    column, lane = iota((width, 2 * DH), 0) % DH, iota((width, 2 * DH), 1)
    left = (lane == column).astype(BF)
    right = (lane == column + DH).astype(BF)
    packed = (dot(kv, left, NN) + dot(qg, right, NN)).astype(BF)
    slices = out_ref.shape[0]
    size = width // slices
    for j in range(slices):
        out_ref[j] = packed[j * size : (j + 1) * size]


def scan_kernel(planes_ref, blocks_ref, out_ref):
    planes, blocks, size = planes_ref.shape[0], blocks_ref.shape[0], blocks_ref.shape[1]
    mine = lax.div(lax.axis_index("seq"), jnp.int32(blocks))
    first = iota((size, 2 * DH), 1) < DH
    zero = jnp.zeros((size, 2 * DH), F32)
    before, after, whole = zero, zero, zero
    for k in range(planes):
        term = planes_ref[k].astype(F32)
        before = before + jnp.where(k < mine, term, 0.0)
        after = after + jnp.where(k > mine, term, 0.0)
        whole = whole + term
    ahead = [before]
    for k in range(blocks - 1):
        ahead.append(ahead[k] + blocks_ref[k].astype(F32))
    behind = [after]
    for k in range(blocks - 1, 0, -1):
        behind.append(behind[-1] + blocks_ref[k].astype(F32))
    behind = behind[::-1]
    for k in range(blocks):
        out_ref[k, :size] = jnp.where(first, ahead[k], behind[k]).astype(BF)
        out_ref[k, size:] = whole.astype(BF)


def attend_kernel(
    scale,
    got_ref,
    state_ref,
    proj_ref,
    grad_ref,
    low_ref,
    up_ref,
    wd_ref,
    dg_ref,
    att_ref,
    gstate_ref,
    part_ref,
    gup_ref,
):
    slices, size = got_ref.shape[0], got_ref.shape[1] // 2
    rows, width = grad_ref.shape
    heads = width // DH
    sums = jnp.concatenate([got_ref[j, :size] for j in range(slices)], axis=0)
    wholes = jnp.concatenate([got_ref[j, size:] for j in range(slices)], axis=0)
    lane, column = iota((2 * DH, DH), 0), iota((2 * DH, DH), 1)
    tail = (lane == column + DH).astype(BF)
    gstate_ref[...] = dot(wholes, tail, NN)
    state = (sums[:, :DH].astype(F32) + state_ref[...]).astype(BF)
    lane, column = iota((DH, width), 0), iota((DH, width), 1) % DH
    head_spread = (lane == column).astype(BF)
    lane, column = iota((2 * DH, width), 0), iota((2 * DH, width), 1) % DH
    tail_spread = (lane == column + DH).astype(BF)
    same = iota((width, width), 0) // DH == iota((width, width), 1) // DH
    state_low = jnp.where(same, dot(state, head_spread, NN), 0.0).astype(BF)
    later_low = jnp.where(same, dot(sums, tail_spread, NN), 0.0).astype(BF)
    query, key, value, grad = proj_ref[0], proj_ref[1], proj_ref[2], grad_ref[...]
    query_s, key_s, value_s, grad_s = per_head(query), per_head(key), per_head(value), per_head(grad)
    row, col = iota((rows, heads * rows), 0), iota((rows, heads * rows), 1) % rows
    lower, upper = col <= row, col >= row
    weights = jnp.where(lower, dot(query, key_s, NT), 0.0).astype(BF)
    weights_t = jnp.where(upper, dot(key, query_s, NT), 0.0).astype(BF)
    dweights = jnp.where(lower, dot(grad, value_s, NT), 0.0).astype(BF)
    dweights_t = jnp.where(upper, dot(value, grad_s, NT), 0.0).astype(BF)
    attended = (scale * (dot(weights, value_s, NN) + dot(query, state_low, NN))).astype(BF)
    att_ref[...] = attended
    back = (
        (dot(dweights, key_s, NN) + dot(grad, state_low, NT)).astype(BF),
        (dot(dweights_t, query_s, NN) + dot(value, later_low, NT)).astype(BF),
        (dot(weights_t, grad_s, NN) + dot(key, later_low, NN)).astype(BF),
    )
    parts = []
    for i in range(3):
        parts.append(dot(up_ref[i], back[i], NT))
        gup_ref[i * RANK : (i + 1) * RANK] = dot(low_ref[i * RANK : (i + 1) * RANK], back[i], NN).astype(BF)
    parts.append(dot(wd_ref[...], attended, NT))
    gup_ref[3 * RANK :] = dot(dg_ref[...], attended, NN).astype(BF)
    fill(part_ref, jnp.concatenate(parts, axis=0).astype(BF))


def layout(slices, model, cols, width):
    lanes = 128
    out_up = RANK * model // (slices * lanes)
    ups = 4 * RANK * width // (slices * lanes)
    down = 3 * RANK * cols // (slices * lanes)
    return out_up, ups, down


def pieces(slices, model, cols, width):
    out_up, ups, down = layout(slices, model, cols, width)
    span = model // slices
    up_rows = 4 * RANK // slices
    half = 3 * RANK // 2
    units = [(r * half, c * 128) for c in range(cols // 128) for r in range(2)]
    each = len(units) // slices
    found = []
    for j in range(slices):
        for c in range(span // 128):
            found.append((j, c * RANK, RANK, "o", 0, j * span + c * 128))
        for c in range(width // 128):
            for r in range(0, up_rows, 8):
                found.append((j, out_up + c * up_rows + r, 8, "u", j * up_rows + r, c * 128))
        for n in range(each):
            found.append((j, out_up + ups + n * half, half, "d", *units[j * each + n]))
    return found


def grads_kernel(got_ref, x_ref, og_ref, gup_ref, out_ref):
    low = total(got_ref).astype(BF)
    down = dot(low[: 3 * RANK], x_ref[...], NN).astype(BF)
    out_up = dot(low[3 * RANK :], og_ref[...], NN).astype(BF)
    kept = {"o": out_up, "u": gup_ref[...], "d": down}
    for j, at, count, name, row, col in pieces(out_ref.shape[0], og_ref.shape[1], x_ref.shape[1], gup_ref.shape[1]):
        out_ref[j, at : at + count] = kept[name][row : row + count, col : col + 128]


def unpack_kernel(got_ref, down_ref, up_ref, odown_ref, oup_ref):
    slices, model, cols, width = got_ref.shape[0], oup_ref.shape[1], down_ref.shape[1], up_ref.shape[1]
    for j, at, count, name, row, col in pieces(slices, model, cols, width):
        value = got_ref[j, at : at + count].astype(F32)
        if name == "o":
            oup_ref[row : row + count, col : col + 128] = value
        elif name == "d":
            down_ref[row : row + count, col : col + 128] = value
        elif row < 3 * RANK:
            up_ref[row : row + count, col : col + 128] = value
        else:
            odown_ref[row - 3 * RANK : row - 3 * RANK + count, col : col + 128] = value


def run(kernel, outs, *args, limit=16 << 20, cost=None):
    vmem = pl.BlockSpec(memory_space=pltpu.VMEM)
    return pl.pallas_call(
        kernel,
        out_shape=[jax.ShapeDtypeStruct(shape, dtype) for shape, dtype in outs],
        in_specs=[vmem] * len(args),
        out_specs=[vmem] * len(outs),
        compiler_params=pltpu.CompilerParams(vmem_limit_bytes=limit),
        cost_estimate=cost,
    )(*args)


def on_device(y_size, z_size, tp_size, inputs, frozen, down_maps, up_maps, state, w_out, down_out, up_out, out_grad):
    rows, cols = inputs.shape
    width, model = frozen.shape[2], out_grad.shape[1]
    scale = 1.0 / math.sqrt(DH * rows * y_size * z_size)
    planes = [[z * y_size + y for y in range(y_size)] for z in range(z_size)]
    columns = [[z * y_size + y for z in range(z_size)] for y in range(y_size)]

    def over_y(a):
        return lax.all_to_all(a, "seq", 0, 0, axis_index_groups=planes)

    def over_z(a):
        return lax.all_to_all(a, "seq", 0, 0, axis_index_groups=columns)

    def over_tp(a):
        return lax.all_to_all(a, "tp", 0, 0)

    down_t = jnp.transpose(down_maps, (0, 2, 1)).reshape(3 * RANK, cols)
    wd_t = down_out.T

    (low_part,) = run(low_kernel, [((tp_size, 3 * RANK, rows), BF)], inputs, down_t, cost=pl.CostEstimate(flops=20_000_000_000, bytes_accessed=1_000_000, transcendentals=0))
    low, proj, grad, down_grad, own = run(
        functools.partial(project_kernel, scale),
        [
            ((3 * RANK, rows), BF),
            ((3, rows, width), BF),
            ((rows, width), BF),
            ((RANK, rows), BF),
            ((y_size, width // y_size, 2 * DH), BF),
        ],
        over_tp(low_part),
        frozen,
        up_maps,
        out_grad,
        w_out,
        wd_t,
        up_out,
    )
    blocks = over_y(own)
    slice_rows = width // y_size
    (plane,) = run(sum_spread_kernel, [((z_size, slice_rows, 2 * DH), BF)], blocks)
    (sums,) = run(scan_kernel, [((y_size, 2 * slice_rows, 2 * DH), BF)], over_z(plane), blocks)
    attended, grad_state, parts, grad_up = run(
        functools.partial(attend_kernel, scale),
        [
            ((rows, width), BF),
            ((width, DH), F32),
            ((tp_size, 4 * RANK, rows), BF),
            ((4 * RANK, width), BF),
        ],
        over_y(sums),
        state.reshape(width, DH),
        proj,
        grad,
        low,
        up_maps,
        wd_t,
        down_grad,
    )
    lines = sum(layout(y_size, model, cols, width))
    (shares,) = run(grads_kernel, [((y_size, lines, 128), BF)], over_tp(parts), inputs, out_grad, grad_up)
    (mine,) = run(sum_spread_kernel, [((z_size, lines, 128), BF)], over_y(shares))
    (whole,) = run(sum_spread_kernel, [((y_size, lines, 128), BF)], over_z(mine))
    down_g, up_g, odown_g, oup_g = run(
        unpack_kernel,
        [((3 * RANK, cols), F32), ((3 * RANK, width), F32), ((RANK, width), F32), ((RANK, model), F32)],
        over_y(whole),
    )
    return (
        attended,
        jnp.transpose(down_g.reshape(3, RANK, cols), (0, 2, 1)),
        up_g.reshape(3, RANK, width),
        odown_g.T,
        oup_g,
        grad_state.reshape(width // DH, DH, DH),
    )


def solution(mesh):
    placed = (
        P("seq", "tp"),
        P(None, "seq", "tp"),
        P(None, "tp", None),
        P(None, None, "tp"),
        P("tp", None, None),
        P("tp", None),
        P("tp", None),
        P(),
        P("seq", None),
    )
    seq, tp = mesh.shape["seq"], mesh.shape["tp"]
    return jax.shard_map(
        functools.partial(on_device, Y_SIZE, seq // Y_SIZE, tp),
        mesh=mesh,
        in_specs=placed,
        out_specs=(
            P("seq", "tp"),
            P(None, "tp", None),
            P(None, None, "tp"),
            P("tp", None),
            P(),
            P("tp", None, None),
        ),
        check_vma=False,
    )
```

```python
import functools
import math

import jax
import jax.numpy as jnp
from jax import lax
from jax.experimental import pallas as pl
from jax.experimental.pallas import tpu as pltpu
from jax.sharding import PartitionSpec as P

DH = 64
RANK = 16
Y_SIZE = 8
BF = jnp.bfloat16
F32 = jnp.float32


def dot(a, b, contract):
    return lax.dot_general(a, b, ((contract[:1], contract[1:]), ((), ())), preferred_element_type=F32)


NN, NT, TN = (1, 0), (1, 1), (0, 0)


def iota(shape, axis):
    return lax.broadcasted_iota(jnp.int32, shape, axis)


def total(ref):
    acc = ref[0].astype(F32)
    for k in range(1, ref.shape[0]):
        acc = acc + ref[k].astype(F32)
    return acc


def fill(ref, value):
    for k in range(ref.shape[0]):
        ref[k] = value


def sum_spread_kernel(in_ref, out_ref):
    fill(out_ref, total(in_ref).astype(BF))


def low_kernel(x_hbm, down_hbm, out_ref, x_ref, down_ref, x_sem, down_sem):
    x_copy = pltpu.make_async_copy(x_hbm, x_ref, x_sem)
    down_copy = pltpu.make_async_copy(down_hbm, down_ref, down_sem)
    x_copy.start()
    down_copy.start()
    x_copy.wait()
    down_copy.wait()
    fill(out_ref, dot(down_ref[...], x_ref[...], NT).astype(BF))


def per_head(rows):
    count, width = rows.shape
    lane = iota((count, width), 1) // DH
    return jnp.concatenate([jnp.where(lane == h, rows, jnp.zeros_like(rows)) for h in range(width // DH)], axis=0)


def project_kernel(
    scale, got_ref, frozen_ref, up_ref, og_ref, w_ref, wd_ref, oup_ref, low_ref, proj_ref, grad_ref, dg_ref, out_ref
):
    width = frozen_ref.shape[2]
    down_grad = dot(oup_ref[...], og_ref[...], NT).astype(BF)
    dg_ref[...] = down_grad
    through = dot(og_ref[...], w_ref[...], NT) + dot(down_grad, wd_ref[...], TN)
    grad = (scale * through).astype(BF)
    grad_ref[...] = grad
    low = total(got_ref).astype(BF)
    low_ref[...] = low
    rows = []
    for i in range(3):
        part = frozen_ref[i].astype(F32) + dot(low[i * RANK : (i + 1) * RANK], up_ref[i], TN)
        rows.append(part.astype(BF))
        proj_ref[i] = rows[i]
    query, key, value = rows
    same = iota((width, width), 0) // DH == iota((width, width), 1) // DH
    kv = jnp.where(same, dot(key, value, TN), 0.0).astype(BF)
    qg = jnp.where(same, dot(query, grad, TN), 0.0).astype(BF)
    column, lane = iota((width, 2 * DH), 0) % DH, iota((width, 2 * DH), 1)
    left = (lane == column).astype(BF)
    right = (lane == column + DH).astype(BF)
    packed = (dot(kv, left, NN) + dot(qg, right, NN)).astype(BF)
    slices = out_ref.shape[0]
    size = width // slices
    for j in range(slices):
        out_ref[j] = packed[j * size : (j + 1) * size]


def scan_kernel(planes_ref, blocks_ref, out_ref):
    planes, blocks, size = planes_ref.shape[0], blocks_ref.shape[0], blocks_ref.shape[1]
    mine = lax.div(lax.axis_index("seq"), jnp.int32(blocks))
    first = iota((size, 2 * DH), 1) < DH
    zero = jnp.zeros((size, 2 * DH), F32)
    before, after, whole = zero, zero, zero
    for k in range(planes):
        term = planes_ref[k].astype(F32)
        before = before + jnp.where(k < mine, term, 0.0)
        after = after + jnp.where(k > mine, term, 0.0)
        whole = whole + term
    ahead = [before]
    for k in range(blocks - 1):
        ahead.append(ahead[k] + blocks_ref[k].astype(F32))
    behind = [after]
    for k in range(blocks - 1, 0, -1):
        behind.append(behind[-1] + blocks_ref[k].astype(F32))
    behind = behind[::-1]
    half = size // 2
    turned = jnp.where(first[:half], pltpu.roll(whole[:half], DH, 1), whole[half:]).astype(BF)
    for k in range(blocks):
        out_ref[k, :size] = jnp.where(first, ahead[k], behind[k]).astype(BF)
        out_ref[k, size:] = turned


def attend_kernel(
    scale,
    got_ref,
    state_ref,
    proj_ref,
    grad_ref,
    low_ref,
    up_ref,
    wd_ref,
    dg_ref,
    att_ref,
    part_ref,
    gup_ref,
):
    slices, size = got_ref.shape[0], got_ref.shape[1] * 2 // 3
    rows, width = grad_ref.shape
    heads = width // DH
    sums = jnp.concatenate([got_ref[j, :size] for j in range(slices)], axis=0)
    state = (sums[:, :DH].astype(F32) + state_ref[...]).astype(BF)
    lane, column = iota((DH, width), 0), iota((DH, width), 1) % DH
    head_spread = (lane == column).astype(BF)
    lane, column = iota((2 * DH, width), 0), iota((2 * DH, width), 1) % DH
    tail_spread = (lane == column + DH).astype(BF)
    same = iota((width, width), 0) // DH == iota((width, width), 1) // DH
    state_low = jnp.where(same, dot(state, head_spread, NN), 0.0).astype(BF)
    later_low = jnp.where(same, dot(sums, tail_spread, NN), 0.0).astype(BF)
    query, key, value, grad = proj_ref[0], proj_ref[1], proj_ref[2], grad_ref[...]
    query_s, key_s, value_s, grad_s = per_head(query), per_head(key), per_head(value), per_head(grad)
    row, col = iota((rows, heads * rows), 0), iota((rows, heads * rows), 1) % rows
    lower, upper = col <= row, col >= row
    weights = jnp.where(lower, dot(query, key_s, NT), 0.0).astype(BF)
    weights_t = jnp.where(upper, dot(key, query_s, NT), 0.0).astype(BF)
    dweights = jnp.where(lower, dot(grad, value_s, NT), 0.0).astype(BF)
    dweights_t = jnp.where(upper, dot(value, grad_s, NT), 0.0).astype(BF)
    attended = (scale * (dot(weights, value_s, NN) + dot(query, state_low, NN))).astype(BF)
    att_ref[...] = attended
    back = (
        (dot(dweights, key_s, NN) + dot(grad, state_low, NT)).astype(BF),
        (dot(dweights_t, query_s, NN) + dot(value, later_low, NT)).astype(BF),
        (dot(weights_t, grad_s, NN) + dot(key, later_low, NN)).astype(BF),
    )
    parts = []
    for i in range(3):
        parts.append(dot(up_ref[i], back[i], NT))
        gup_ref[i * RANK : (i + 1) * RANK] = dot(low_ref[i * RANK : (i + 1) * RANK], back[i], NN).astype(BF)
    parts.append(dot(wd_ref[...], attended, NT))
    gup_ref[3 * RANK :] = dot(dg_ref[...], attended, NN).astype(BF)
    fill(part_ref, jnp.concatenate(parts, axis=0).astype(BF))


def layout(slices, model, cols, width):
    lanes = 128
    out_up = RANK * model // (slices * lanes)
    ups = 4 * RANK * width // (slices * lanes)
    down = 3 * RANK * cols // (slices * lanes)
    return out_up, ups, down


def pieces(slices, model, cols, width):
    out_up, ups, down = layout(slices, model, cols, width)
    span = model // slices
    up_rows = 4 * RANK // slices
    half = 3 * RANK // 2
    units = [(r * half, c * 128) for c in range(cols // 128) for r in range(2)]
    each = len(units) // slices
    found = []
    for j in range(slices):
        for c in range(span // 128):
            found.append((j, c * RANK, RANK, "o", 0, j * span + c * 128))
        for c in range(width // 128):
            for r in range(0, up_rows, 8):
                found.append((j, out_up + c * up_rows + r, 8, "u", j * up_rows + r, c * 128))
        for n in range(each):
            found.append((j, out_up + ups + n * half, half, "d", *units[j * each + n]))
    return found


def grads_kernel(got_ref, x_ref, og_ref, gup_ref, out_ref):
    low = total(got_ref).astype(BF)
    down = dot(low[: 3 * RANK], x_ref[...], NN).astype(BF)
    out_up = dot(low[3 * RANK :], og_ref[...], NN).astype(BF)
    kept = {"o": out_up, "u": gup_ref[...], "d": down}
    for j, at, count, name, row, col in pieces(out_ref.shape[0], og_ref.shape[1], x_ref.shape[1], gup_ref.shape[1]):
        out_ref[j, at : at + count] = kept[name][row : row + count, col : col + 128]


def unpack_kernel(got_ref, sums_ref, att_ref, down_ref, up_ref, odown_ref, oup_ref, state_ref, attended_ref):
    attended_ref[...] = att_ref[...]
    half = sums_ref.shape[1] // 3
    for j in range(sums_ref.shape[0]):
        both = sums_ref[j, 2 * half :].astype(F32)
        state_ref[2 * half * j : 2 * half * j + half] = both[:, :DH]
        state_ref[2 * half * j + half : 2 * half * (j + 1)] = pltpu.roll(both, DH, 1)[:, :DH]
    slices, model, cols, width = got_ref.shape[0], oup_ref.shape[1], down_ref.shape[1], up_ref.shape[1]
    for j, at, count, name, row, col in pieces(slices, model, cols, width):
        value = got_ref[j, at : at + count].astype(F32)
        if name == "o":
            oup_ref[row : row + count, col : col + 128] = value
        elif name == "d":
            down_ref[row : row + count, col : col + 128] = value
        elif row < 3 * RANK:
            up_ref[row : row + count, col : col + 128] = value
        else:
            odown_ref[row - 3 * RANK : row - 3 * RANK + count, col : col + 128] = value


def run(kernel, outs, *args, limit=16 << 20, cost=None):
    vmem = pl.BlockSpec(memory_space=pltpu.VMEM)
    return pl.pallas_call(
        kernel,
        out_shape=[jax.ShapeDtypeStruct(shape, dtype) for shape, dtype in outs],
        in_specs=[vmem] * len(args),
        out_specs=[vmem] * len(outs),
        compiler_params=pltpu.CompilerParams(vmem_limit_bytes=limit),
        cost_estimate=cost,
    )(*args)


def on_device(y_size, z_size, tp_size, inputs, frozen, down_maps, up_maps, state, w_out, down_out, up_out, out_grad):
    rows, cols = inputs.shape
    width, model = frozen.shape[2], out_grad.shape[1]
    scale = 1.0 / math.sqrt(DH * rows * y_size * z_size)
    planes = [[z * y_size + y for y in range(y_size)] for z in range(z_size)]
    columns = [[z * y_size + y for z in range(z_size)] for y in range(y_size)]

    def over_y(a):
        return lax.all_to_all(a, "seq", 0, 0, axis_index_groups=planes)

    def over_z(a):
        return lax.all_to_all(a, "seq", 0, 0, axis_index_groups=columns)

    def over_tp(a):
        return lax.all_to_all(a, "tp", 0, 0)

    down_t = jnp.transpose(down_maps, (0, 2, 1)).reshape(3 * RANK, cols)
    wd_t = down_out.T

    hbm = pl.BlockSpec(memory_space=pltpu.HBM)
    low_part = pl.pallas_call(
        low_kernel,
        out_shape=jax.ShapeDtypeStruct((tp_size, 3 * RANK, rows), BF),
        in_specs=[hbm, hbm],
        out_specs=pl.BlockSpec(memory_space=pltpu.VMEM),
        scratch_shapes=[
            pltpu.VMEM((rows, cols), BF),
            pltpu.VMEM((3 * RANK, cols), BF),
            pltpu.SemaphoreType.DMA,
            pltpu.SemaphoreType.DMA,
        ],
        compiler_params=pltpu.CompilerParams(vmem_limit_bytes=4 << 20),
        cost_estimate=pl.CostEstimate(flops=20_000_000_000, bytes_accessed=1_000_000, transcendentals=0),
    )(pltpu.with_memory_space_constraint(inputs, pltpu.HBM), pltpu.with_memory_space_constraint(down_t, pltpu.HBM))
    low, proj, grad, down_grad, own = run(
        functools.partial(project_kernel, scale),
        [
            ((3 * RANK, rows), BF),
            ((3, rows, width), BF),
            ((rows, width), BF),
            ((RANK, rows), BF),
            ((y_size, width // y_size, 2 * DH), BF),
        ],
        over_tp(low_part),
        frozen,
        up_maps,
        out_grad,
        w_out,
        wd_t,
        up_out,
    )
    blocks = over_y(own)
    slice_rows = width // y_size
    (plane,) = run(sum_spread_kernel, [((z_size, slice_rows, 2 * DH), BF)], blocks)
    (sums,) = run(scan_kernel, [((y_size, 3 * slice_rows // 2, 2 * DH), BF)], over_z(plane), blocks)
    sums = over_y(sums)
    attended, parts, grad_up = run(
        functools.partial(attend_kernel, scale),
        [
            ((rows, width), BF),
            ((tp_size, 4 * RANK, rows), BF),
            ((4 * RANK, width), BF),
        ],
        sums,
        state.reshape(width, DH),
        proj,
        grad,
        low,
        up_maps,
        wd_t,
        down_grad,
    )
    lines = sum(layout(y_size, model, cols, width))
    (shares,) = run(grads_kernel, [((y_size, lines, 128), BF)], over_tp(parts), inputs, out_grad, grad_up)
    (mine,) = run(sum_spread_kernel, [((z_size, lines, 128), BF)], over_y(shares))
    (whole,) = run(sum_spread_kernel, [((y_size, lines, 128), BF)], over_z(mine))
    down_g, up_g, odown_g, oup_g, grad_state, attended = run(
        unpack_kernel,
        [
            ((3 * RANK, cols), F32),
            ((3 * RANK, width), F32),
            ((RANK, width), F32),
            ((RANK, model), F32),
            ((width, DH), F32),
            ((rows, width), BF),
        ],
        over_y(whole),
        sums,
        attended,
    )
    return (
        attended,
        jnp.transpose(down_g.reshape(3, RANK, cols), (0, 2, 1)),
        up_g.reshape(3, RANK, width),
        odown_g.T,
        oup_g,
        grad_state.reshape(width // DH, DH, DH),
    )


def solution(mesh):
    placed = (
        P("seq", "tp"),
        P(None, "seq", "tp"),
        P(None, "tp", None),
        P(None, None, "tp"),
        P("tp", None, None),
        P("tp", None),
        P("tp", None),
        P(),
        P("seq", None),
    )
    seq, tp = mesh.shape["seq"], mesh.shape["tp"]
    return jax.shard_map(
        functools.partial(on_device, Y_SIZE, seq // Y_SIZE, tp),
        mesh=mesh,
        in_specs=placed,
        out_specs=(
            P("seq", "tp"),
            P(None, "tp", None),
            P(None, None, "tp"),
            P("tp", None),
            P(),
            P("tp", None, None),
        ),
        check_vma=False,
    )
```
